256 devices in a mesh: dp: 16 (over x, y_hi, core), expert: 16 (over y_lo, z).
Axes of the slice: x: 4, y: 4 (y_hi: 2, y_lo: 2; y = y_hi * 2 + y_lo), z: 8, core: 2. Of those that a mesh axis runs over, the one named last changes fastest.
Arguments:
- tokens: bfloat16 [2048, 7168], P('dp', 'expert'), may hold values from -6 to 6
- grad_out: bfloat16 [2048, 7168], P('dp', 'expert'), may hold values from -6 to 6
- w_gate: bfloat16 [16, 7168, 2048], P('dp', None, 'expert'), may hold values from -0.0625 to 0.0625
- w_up: bfloat16 [16, 7168, 2048], P('dp', None, 'expert'), may hold values from -0.0625 to 0.0625
- w_down: bfloat16 [16, 2048, 7168], P('dp', 'expert'), may hold values from -0.125 to 0.125
- routing: int32 [2048, 2], replicated, may hold values from 0 to 15, as said below
- combine: float32 [2048, 2], replicated, may hold values from 0.2 to 1
- hot_ids: int32 [16], replicated, may hold values from 0 to 15, as said below
Outputs:
- grad_gate: bfloat16 [16, 7168, 2048], P('dp', None, 'expert')
- grad_up: bfloat16 [16, 7168, 2048], P('dp', None, 'expert')
- grad_down: bfloat16 [16, 2048, 7168], P('dp', 'expert')
- grad_tokens: bfloat16 [2048, 7168], P('dp', 'expert')
The draws below stay inside these ranges and needn't reach their ends.
Inputs may be any that keep to these rules, and one draw needn't show every extreme that they name: `routing`: each token names 2 different experts. `hot_ids`: a permutation of the 16 experts.
All inputs are finite; a program needn't handle non-finite values.
Results may differ from the reference program's by a relative error of at most 0.018.
Values may be sent and summed in bfloat16 or wider, within the bound.
A program may use at most 128 MiB of HBM per device.

```python
import jax
import jax.numpy as jnp
from jax import lax

D = 7168
FF = 2048
TOKR = 128
TOP = 2
EXPERTS = 16
CAP = 16
TOKENS = 2048
N_DP = 16
N_EXPERT = 16


def ranked_experts(key):
    return jax.random.permutation(jax.random.fold_in(key, 7), EXPERTS).astype(jnp.int32)


def draw_hot_ids(key, part):
    return ranked_experts(key)


def draw_routing(key, part):
    hot_expert = ranked_experts(key)[0]
    scores = jax.random.randint(jax.random.fold_in(key, 11), (TOKENS, EXPERTS), 0, 2 ** 20)
    columns = jnp.arange(EXPERTS, dtype=jnp.int32)
    scores = scores + jnp.where(columns[None, :] == hot_expert, 2 ** 19, 0)
    scores = scores * EXPERTS + columns[None, :]
    return lax.top_k(scores, TOP)[1].astype(jnp.int32)


def steps_of(stream_key, extent, cuts, least, top_value):
    gain, own = 1.0, jax.random.fold_in(stream_key, 6)
    for axis_at, shards_of in cuts:
        draws = jnp.exp(jax.random.uniform(jax.random.fold_in(own, axis_at), (shards_of,), jnp.float32, least / len(cuts), top_value / len(cuts)))
        gain = gain * jnp.repeat(draws, extent[axis_at] // shards_of).reshape([-1 if axis == axis_at else 1 for axis in range(len(extent))])
    return gain


def gaussian(key, extent, scale, most, split=(), held_as=jnp.bfloat16):
    gain = steps_of(key, extent, split, -0.22, 0.18) if split else 1.0
    values = jax.random.normal(key, extent, jnp.float32) * scale * gain
    return jnp.minimum(jnp.maximum(values, -most), most).astype(held_as)


def setup_inputs(seed: int = 0) -> dict:
    streams_of = jax.random.split(jax.random.key(seed), 9)
    return {
        "tokens": gaussian(streams_of[0], (TOKENS, D), 1.0, 6.0, ((0, 16), (1, 16))),
        "grad_out": gaussian(streams_of[1], (TOKENS, D), 1.0, 6.0, ((0, 16), (1, 16))),
        "w_gate": gaussian(streams_of[2], (EXPERTS, D, FF), D ** -0.5, 0.0625, ((0, 16), (2, 16))),
        "w_up": gaussian(streams_of[3], (EXPERTS, D, FF), D ** -0.5, 0.0625, ((0, 16), (2, 16))),
        "w_down": gaussian(streams_of[4], (EXPERTS, FF, D), FF ** -0.5, 0.125, ((0, 16), (1, 16))),
        "routing": draw_routing(jax.random.fold_in(streams_of[8], 71), 0),
        "combine": jnp.clip(jax.random.uniform(streams_of[6], (TOKENS, TOP), jnp.float32, 0.2, 1.0), 0.2, 1.0),
        "hot_ids": draw_hot_ids(jax.random.fold_in(streams_of[8], 71), 0),
    }


def slot_tables(routing, combine, hot_expert, dp_count, block_rows, expert_count, capacity):
    columns = jnp.arange(expert_count, dtype=jnp.int32)
    name_match = routing[:, :, None] == columns[None, None, :]
    route_weight = jnp.sum(jnp.where(name_match, combine[:, :, None], jnp.float32(0.0)), axis=1)
    named_count = jnp.sum(name_match.astype(jnp.int32), axis=1).reshape(dp_count, block_rows, expert_count)
    before = jnp.cumsum(named_count, axis=1) - named_count
    slot_ids = jnp.arange(capacity, dtype=jnp.int32)
    slot_match = (named_count[..., None] == 1) & (before[..., None] == slot_ids) & (columns != hot_expert)[None, None, :, None]
    positions = jnp.arange(block_rows, dtype=jnp.int32)
    slot_token = jnp.sum(jnp.where(slot_match, positions[None, :, None, None], 0), axis=1).astype(jnp.int32)
    slot_live = jnp.any(slot_match, axis=1)
    return route_weight, slot_token, slot_live


def expert_terms(rows_in, rows_back, weight, gate_cols, up_cols, down_rows):
    gate_pre = jnp.dot(rows_in, gate_cols, preferred_element_type=jnp.float32)
    up_pre = jnp.dot(rows_in, up_cols, preferred_element_type=jnp.float32)
    sigmoid_gate = jax.nn.sigmoid(gate_pre)
    active = gate_pre * sigmoid_gate
    back_hidden = weight[:, None] * jnp.dot(rows_back, down_rows.T, preferred_element_type=jnp.float32)
    scaled = (weight[:, None] * active * up_pre).astype(jnp.bfloat16)
    grad_gate_pre = (back_hidden * up_pre * sigmoid_gate * (1.0 + gate_pre * (1.0 - sigmoid_gate))).astype(jnp.bfloat16)
    grad_up_pre = (back_hidden * active).astype(jnp.bfloat16)
    gate_sum = jnp.dot(rows_in.T, grad_gate_pre, preferred_element_type=jnp.float32)
    up_sum = jnp.dot(rows_in.T, grad_up_pre, preferred_element_type=jnp.float32)
    down_sum = jnp.dot(scaled.T, rows_back, preferred_element_type=jnp.float32)
    row_count = rows_in.shape[0]
    hidden_group = FF // N_EXPERT
    gate_groups = grad_gate_pre.astype(jnp.float32).reshape(row_count, N_EXPERT, hidden_group)
    up_groups = grad_up_pre.astype(jnp.float32).reshape(row_count, N_EXPERT, hidden_group)
    gate_blocks = gate_cols.astype(jnp.float32).reshape(D, N_EXPERT, hidden_group)
    up_blocks = up_cols.astype(jnp.float32).reshape(D, N_EXPERT, hidden_group)
    group_terms = jnp.einsum("rgh,dgh->rgd", gate_groups, gate_blocks) + jnp.einsum("rgh,dgh->rgd", up_groups, up_blocks)
    rounded = lax.optimization_barrier(group_terms.astype(jnp.bfloat16))
    back = jnp.sum(rounded.astype(jnp.float32), axis=1)
    return gate_sum, up_sum, down_sum, back


def reference(tokens, grad_out, w_gate, w_up, w_down, routing, combine, hot_ids):
    hot_expert = hot_ids[0]
    route_weight, slot_token, slot_live = slot_tables(routing, combine, hot_expert, N_DP, TOKR, EXPERTS, CAP)
    offsets = (jnp.arange(N_DP, dtype=jnp.int32) * TOKR)[:, None, None]
    global_token = (slot_token + offsets).astype(jnp.int32)

    def cold_expert(expert_id):
        token_ids = global_token[:, expert_id, :].reshape(-1)
        live = slot_live[:, expert_id, :].reshape(-1)
        weight = jnp.where(live, route_weight[token_ids, expert_id], jnp.float32(0.0))
        terms = expert_terms(tokens[token_ids], grad_out[token_ids], weight, w_gate[expert_id], w_up[expert_id], w_down[expert_id])
        return terms[0].astype(jnp.bfloat16), terms[1].astype(jnp.bfloat16), terms[2].astype(jnp.bfloat16), terms[3]

    cold_gate, cold_up, cold_down, cold_back = lax.map(cold_expert, jnp.arange(EXPERTS, dtype=jnp.int32))

    hot_gate_w = w_gate[hot_expert]
    hot_up_w = w_up[hot_expert]
    hot_down_w = w_down[hot_expert]
    hot_column = route_weight[:, hot_expert]

    def hot_step(carry, block_index):
        start = (block_index * TOKR).astype(jnp.int32)
        rows_in = lax.dynamic_slice_in_dim(tokens, start, TOKR, 0)
        rows_back = lax.dynamic_slice_in_dim(grad_out, start, TOKR, 0)
        weight = lax.dynamic_slice_in_dim(hot_column, start, TOKR, 0)
        terms = expert_terms(rows_in, rows_back, weight, hot_gate_w, hot_up_w, hot_down_w)
        updated = tuple(carry[member] + lax.optimization_barrier(terms[member].astype(jnp.bfloat16)).astype(jnp.float32) for member in range(3))
        return updated, terms[3]

    start_carry = (jnp.zeros((D, FF), jnp.float32), jnp.zeros((D, FF), jnp.float32), jnp.zeros((FF, D), jnp.float32))
    hot_sums, hot_back = lax.scan(hot_step, start_carry, jnp.arange(N_DP, dtype=jnp.int32))
    grad_gate = cold_gate.at[hot_expert].set(hot_sums[0].astype(jnp.bfloat16))
    grad_up = cold_up.at[hot_expert].set(hot_sums[1].astype(jnp.bfloat16))
    grad_down = cold_down.at[hot_expert].set(hot_sums[2].astype(jnp.bfloat16))
    all_tokens = jnp.transpose(global_token, (1, 0, 2)).reshape(-1)
    token_grad = hot_back.reshape(TOKENS, D).at[all_tokens].add(cold_back.reshape(-1, D))
    return grad_gate, grad_up, grad_down, token_grad.astype(jnp.bfloat16)
```

```python
import jax
import jax.numpy as jnp
from jax import lax
from jax.sharding import PartitionSpec as P


def slot_tables(routing, combine, hot_expert, dp_count, block_rows, expert_count, capacity):
    columns = jnp.arange(expert_count, dtype=jnp.int32)
    name_match = routing[:, :, None] == columns[None, None, :]
    route_weight = jnp.sum(jnp.where(name_match, combine[:, :, None], jnp.float32(0.0)), axis=1)
    named_count = jnp.sum(name_match.astype(jnp.int32), axis=1).reshape(
        dp_count, block_rows, expert_count
    )
    before = jnp.cumsum(named_count, axis=1) - named_count
    slot_ids = jnp.arange(capacity, dtype=jnp.int32)
    slot_match = (
        (named_count[..., None] == 1)
        & (before[..., None] == slot_ids)
        & (columns != hot_expert)[None, None, :, None]
    )
    positions = jnp.arange(block_rows, dtype=jnp.int32)
    slot_token = jnp.sum(jnp.where(slot_match, positions[None, :, None, None], 0), axis=1)
    slot_live = jnp.any(slot_match, axis=1)
    return (route_weight, slot_token, slot_live)


def expert_terms(rows_in, rows_back, weight, gate_cols, up_cols, down_cols):
    across = (((1,), (1,)), ((), ()))
    downward = (((0,), (0,)), ((), ()))
    gate_pre = jnp.dot(rows_in, gate_cols, preferred_element_type=jnp.float32)
    up_pre = jnp.dot(rows_in, up_cols, preferred_element_type=jnp.float32)
    sigmoid_gate = jax.nn.sigmoid(gate_pre)
    active = gate_pre * sigmoid_gate
    back_hidden = weight[:, None] * jnp.dot(rows_back, down_cols, preferred_element_type=jnp.float32)
    scaled = (weight[:, None] * active * up_pre).astype(jnp.bfloat16)
    grad_gate_pre = (
        back_hidden * up_pre * sigmoid_gate * (1.0 + gate_pre * (1.0 - sigmoid_gate))
    ).astype(jnp.bfloat16)
    grad_up_pre = (back_hidden * active).astype(jnp.bfloat16)
    gate_sum = lax.dot_general(rows_in, grad_gate_pre, downward, preferred_element_type=jnp.float32)
    up_sum = lax.dot_general(rows_in, grad_up_pre, downward, preferred_element_type=jnp.float32)
    down_sum = lax.dot_general(rows_back, scaled, downward, preferred_element_type=jnp.float32)
    back = lax.dot_general(grad_gate_pre, gate_cols, across, preferred_element_type=jnp.float32)
    back = back + lax.dot_general(grad_up_pre, up_cols, across, preferred_element_type=jnp.float32)
    return (gate_sum, up_sum, down_sum, back)


def on_device(tokens, grad_out, w_gate, w_up, w_down, routing, combine, hot_ids):
    dp_count = lax.axis_size("dp")
    block_rows = tokens.shape[0]
    share_width = tokens.shape[1]
    width = w_gate.shape[1]
    capacity = block_rows * routing.shape[1] // dp_count
    row_index = lax.axis_index("dp")
    hot_expert = hot_ids[0]
    route_weight, slot_token, slot_live = slot_tables(
        routing, combine, hot_expert, dp_count, block_rows, dp_count, capacity
    )
    send_token = slot_token[row_index]
    send_live = slot_live[row_index]
    recv_token = (
        slot_token[:, row_index, :] + (jnp.arange(dp_count, dtype=jnp.int32) * block_rows)[:, None]
    )
    recv_live = slot_live[:, row_index, :]
    cold_weight = jnp.where(
        recv_live, route_weight[recv_token, row_index], jnp.float32(0.0)
    ).reshape(-1)
    block_weight = lax.dynamic_slice_in_dim(route_weight, row_index * block_rows, block_rows, 0)
    hot_weight = block_weight[:, hot_expert]

    own_down_cols = w_down[0].T
    own = jnp.stack([w_gate[0], w_up[0], own_down_cols], 0)
    own = own.reshape(3, dp_count, width // dp_count, own.shape[-1])
    pieces = lax.all_to_all(own, "dp", split_axis=1, concat_axis=1, tiled=True)
    hot_piece = lax.dynamic_index_in_dim(pieces, hot_expert, axis=1, keepdims=False)
    hot_w = lax.all_gather(hot_piece, "dp", axis=1, tiled=True)
    hot_gate_w, hot_up_w, hot_down_cols = hot_w[0], hot_w[1], hot_w[2]

    def pack(source):
        picked = jnp.take(source, send_token.reshape(-1), axis=0).reshape(
            dp_count, capacity, source.shape[1]
        )
        return jnp.where(send_live[:, :, None], picked, jnp.zeros_like(picked))

    packed = jnp.concatenate([pack(tokens), pack(grad_out)], 2)
    arrived = lax.all_to_all(packed, "dp", split_axis=0, concat_axis=0, tiled=True)
    arrived_in = arrived[:, :, :share_width].reshape(-1, share_width)
    arrived_back = arrived[:, :, share_width:].reshape(-1, share_width)
    local = jnp.stack(
        [jnp.concatenate([tokens, arrived_in], 0), jnp.concatenate([grad_out, arrived_back], 0)], 0
    )
    full = lax.all_gather(local, "expert", axis=2, tiled=True)
    full_in, full_back = full[0], full[1]
    hot_rows, cold_rows = (full_in[:block_rows], full_in[block_rows:])
    hot_cotan, cold_cotan = (full_back[:block_rows], full_back[block_rows:])
    cold_terms = expert_terms(
        cold_rows, cold_cotan, cold_weight, w_gate[0], w_up[0], own_down_cols
    )
    hot_terms = expert_terms(hot_rows, hot_cotan, hot_weight, hot_gate_w, hot_up_w, hot_down_cols)

    block_sums = jnp.stack([hot_terms[m].astype(jnp.bfloat16) for m in range(3)], 0)
    block_sums = block_sums.reshape(3, dp_count, width // dp_count, block_sums.shape[-1])
    by_chunk = lax.all_to_all(block_sums, "dp", split_axis=1, concat_axis=1, tiled=True)
    chunk_sum = jnp.sum(by_chunk.astype(jnp.float32), axis=1).astype(jnp.bfloat16)
    summed = lax.all_gather(chunk_sum, "dp", axis=1, tiled=True)
    owns_hot = row_index == hot_expert
    grad_gate = jnp.where(owns_hot, summed[0], cold_terms[0].astype(jnp.bfloat16))
    grad_up = jnp.where(owns_hot, summed[1], cold_terms[1].astype(jnp.bfloat16))
    grad_down = jnp.where(owns_hot, summed[2], cold_terms[2].astype(jnp.bfloat16)).T

    positions = jnp.arange(block_rows, dtype=jnp.int32)
    select = (positions[:, None] == send_token.reshape(-1)[None, :]) & send_live.reshape(-1)[
        None, :
    ]
    stacked = jnp.concatenate([hot_terms[3], cold_terms[3]], 0)
    shares = lax.psum_scatter(
        stacked.astype(jnp.bfloat16), "expert", scatter_dimension=1, tiled=True
    ).astype(jnp.float32)
    hot_share = shares[:block_rows]
    cold_share = shares[block_rows:].reshape(dp_count, capacity, share_width)
    returned = lax.all_to_all(
        cold_share.astype(jnp.bfloat16), "dp", split_axis=0, concat_axis=0, tiled=True
    ).astype(cold_share.dtype)
    gathered_back = jnp.dot(
        select.astype(jnp.float32),
        returned.reshape(-1, share_width),
        precision=lax.Precision.HIGHEST,
        preferred_element_type=jnp.float32,
    )
    token_grad = (hot_share + gathered_back).astype(jnp.bfloat16)
    return (grad_gate[None], grad_up[None], grad_down[None], token_grad)


def solution(mesh):
    return jax.shard_map(
        on_device,
        mesh=mesh,
        in_specs=(
            P("dp", "expert"),
            P("dp", "expert"),
            P("dp", None, "expert"),
            P("dp", None, "expert"),
            P("dp", "expert", None),
            P(),
            P(),
            P(),
        ),
        out_specs=(
            P("dp", None, "expert"),
            P("dp", None, "expert"),
            P("dp", "expert", None),
            P("dp", "expert"),
        ),
        check_vma=False,
    )
```

```python
import jax
import jax.numpy as jnp
from jax import lax
from jax.sharding import PartitionSpec as P


def slot_tables(routing, combine, hot_expert, dp_count, block_rows, expert_count, capacity):
    columns = jnp.arange(expert_count, dtype=jnp.int32)
    name_match = routing[:, :, None] == columns[None, None, :]
    route_weight = jnp.sum(jnp.where(name_match, combine[:, :, None], jnp.float32(0.0)), axis=1)
    named_count = jnp.sum(name_match.astype(jnp.int32), axis=1).reshape(
        dp_count, block_rows, expert_count
    )
    before = jnp.cumsum(named_count, axis=1) - named_count
    slot_ids = jnp.arange(capacity, dtype=jnp.int32)
    slot_match = (
        (named_count[..., None] == 1)
        & (before[..., None] == slot_ids)
        & (columns != hot_expert)[None, None, :, None]
    )
    positions = jnp.arange(block_rows, dtype=jnp.int32)
    slot_token = jnp.sum(jnp.where(slot_match, positions[None, :, None, None], 0), axis=1)
    slot_live = jnp.any(slot_match, axis=1)
    return (route_weight, slot_token, slot_live)


def expert_terms(rows_in, rows_back, weight, gate_cols, up_cols, down_cols):
    gate_pre = jnp.einsum("srk,skh->rh", rows_in, gate_cols, preferred_element_type=jnp.float32)
    up_pre = jnp.einsum("srk,skh->rh", rows_in, up_cols, preferred_element_type=jnp.float32)
    sigmoid_gate = jax.nn.sigmoid(gate_pre)
    active = gate_pre * sigmoid_gate
    back_hidden = weight[:, None] * jnp.einsum(
        "srk,skh->rh", rows_back, down_cols, preferred_element_type=jnp.float32
    )
    scaled = (weight[:, None] * active * up_pre).astype(jnp.bfloat16)
    grad_gate_pre = (
        back_hidden * up_pre * sigmoid_gate * (1.0 + gate_pre * (1.0 - sigmoid_gate))
    ).astype(jnp.bfloat16)
    grad_up_pre = (back_hidden * active).astype(jnp.bfloat16)
    gate_sum = jnp.einsum("srk,rh->skh", rows_in, grad_gate_pre, preferred_element_type=jnp.float32)
    up_sum = jnp.einsum("srk,rh->skh", rows_in, grad_up_pre, preferred_element_type=jnp.float32)
    down_sum = jnp.einsum("srk,rh->skh", rows_back, scaled, preferred_element_type=jnp.float32)
    back = jnp.einsum("rh,skh->srk", grad_gate_pre, gate_cols, preferred_element_type=jnp.float32)
    back = back + jnp.einsum("rh,skh->srk", grad_up_pre, up_cols, preferred_element_type=jnp.float32)
    return (gate_sum, up_sum, down_sum, back)


def on_device(tokens, grad_out, w_gate, w_up, w_down, routing, combine, hot_ids):
    dp_count = lax.axis_size("dp")
    block_rows = tokens.shape[0]
    share_width = tokens.shape[1]
    width = w_gate.shape[1]
    capacity = block_rows * routing.shape[1] // dp_count
    row_index = lax.axis_index("dp")
    hot_expert = hot_ids[0]
    route_weight, slot_token, slot_live = slot_tables(
        routing, combine, hot_expert, dp_count, block_rows, dp_count, capacity
    )
    send_token = slot_token[row_index]
    send_live = slot_live[row_index]
    recv_token = (
        slot_token[:, row_index, :] + (jnp.arange(dp_count, dtype=jnp.int32) * block_rows)[:, None]
    )
    recv_live = slot_live[:, row_index, :]
    cold_weight = jnp.where(
        recv_live, route_weight[recv_token, row_index], jnp.float32(0.0)
    ).reshape(-1)
    block_weight = lax.dynamic_slice_in_dim(route_weight, row_index * block_rows, block_rows, 0)
    hot_weight = block_weight[:, hot_expert]

    share_count = lax.axis_size("expert")
    own = jnp.stack([w_gate[0], w_up[0], w_down[0].T], 0)
    own = own.reshape(3, share_count, width // share_count, own.shape[-1])
    pieces = lax.all_to_all(own, "dp", split_axis=1, concat_axis=1, tiled=True)
    hot_piece = lax.dynamic_index_in_dim(pieces, hot_expert, axis=1, keepdims=False)
    hot_w = lax.all_gather(hot_piece, "dp", axis=1, tiled=True).reshape(own.shape)

    def pack(source):
        picked = jnp.take(source, send_token.reshape(-1), axis=0).reshape(
            dp_count, capacity, source.shape[1]
        )
        return jnp.where(send_live[:, :, None], picked, jnp.zeros_like(picked))

    packed = jnp.concatenate([pack(tokens), pack(grad_out)], 2)
    arrived = lax.all_to_all(packed, "dp", split_axis=0, concat_axis=0, tiled=True)
    arrived_in = arrived[:, :, :share_width].reshape(-1, share_width)
    arrived_back = arrived[:, :, share_width:].reshape(-1, share_width)
    full_in = lax.all_gather(jnp.concatenate([tokens, arrived_in], 0), "expert", axis=0)
    full_back = lax.all_gather(jnp.concatenate([grad_out, arrived_back], 0), "expert", axis=0)
    hot_rows, cold_rows = (full_in[:, :block_rows], full_in[:, block_rows:])
    hot_cotan, cold_cotan = (full_back[:, :block_rows], full_back[:, block_rows:])
    cold_terms = expert_terms(cold_rows, cold_cotan, cold_weight, own[0], own[1], own[2])
    hot_terms = expert_terms(hot_rows, hot_cotan, hot_weight, hot_w[0], hot_w[1], hot_w[2])

    block_sums = jnp.stack([hot_terms[m].astype(jnp.bfloat16) for m in range(3)], 0)
    by_chunk = lax.all_to_all(block_sums, "dp", split_axis=1, concat_axis=1, tiled=True)
    chunk_sum = jnp.sum(by_chunk.astype(jnp.float32), axis=1).astype(jnp.bfloat16)
    summed = lax.all_gather(chunk_sum, "dp", axis=1, tiled=True).reshape(block_sums.shape)
    owns_hot = row_index == hot_expert
    grads = jnp.where(owns_hot, summed, jnp.stack([cold_terms[m] for m in range(3)], 0))
    grads = grads.astype(jnp.bfloat16).reshape(3, width, grads.shape[-1])
    grad_gate, grad_up, grad_down = grads[0], grads[1], grads[2].T

    positions = jnp.arange(block_rows, dtype=jnp.int32)
    select = (positions[:, None] == send_token.reshape(-1)[None, :]) & send_live.reshape(-1)[
        None, :
    ]
    stacked = jnp.concatenate([hot_terms[3], cold_terms[3]], 1)
    shares = lax.psum_scatter(
        stacked.astype(jnp.bfloat16), "expert", scatter_dimension=0, tiled=True
    )[0].astype(jnp.float32)
    hot_share = shares[:block_rows]
    cold_share = shares[block_rows:].reshape(dp_count, capacity, share_width)
    returned = lax.all_to_all(
        cold_share.astype(jnp.bfloat16), "dp", split_axis=0, concat_axis=0, tiled=True
    ).astype(cold_share.dtype)
    gathered_back = jnp.dot(
        select.astype(jnp.float32),
        returned.reshape(-1, share_width),
        precision=lax.Precision.HIGHEST,
        preferred_element_type=jnp.float32,
    )
    token_grad = (hot_share + gathered_back).astype(jnp.bfloat16)
    return (grad_gate[None], grad_up[None], grad_down[None], token_grad)


def solution(mesh):
    return jax.shard_map(
        on_device,
        mesh=mesh,
        in_specs=(
            P("dp", "expert"),
            P("dp", "expert"),
            P("dp", None, "expert"),
            P("dp", None, "expert"),
            P("dp", "expert", None),
            P(),
            P(),
            P(),
        ),
        out_specs=(
            P("dp", None, "expert"),
            P("dp", None, "expert"),
            P("dp", "expert", None),
            P("dp", "expert"),
        ),
        check_vma=False,
    )
```

```python
import jax
import jax.numpy as jnp
from jax import lax
from jax.sharding import PartitionSpec as P


def slot_tables(routing, combine, hot_expert, dp_count, block_rows, expert_count, capacity):
    columns = jnp.arange(expert_count, dtype=jnp.int32)
    name_match = routing[:, :, None] == columns[None, None, :]
    route_weight = jnp.sum(jnp.where(name_match, combine[:, :, None], jnp.float32(0.0)), axis=1)
    named_count = jnp.sum(name_match.astype(jnp.int32), axis=1).reshape(
        dp_count, block_rows, expert_count
    )
    positions = jnp.arange(block_rows, dtype=jnp.int32)
    earlier = (positions[None, :] < positions[:, None]).astype(jnp.bfloat16)
    before = jnp.einsum(
        "ts,bse->bte", earlier, named_count.astype(jnp.bfloat16), preferred_element_type=jnp.float32
    ).astype(jnp.int32)
    slot_ids = jnp.arange(capacity, dtype=jnp.int32)
    slot_match = (
        (named_count[..., None] == 1)
        & (before[..., None] == slot_ids)
        & (columns != hot_expert)[None, None, :, None]
    )
    slot_token = jnp.sum(jnp.where(slot_match, positions[None, :, None, None], 0), axis=1)
    slot_live = jnp.any(slot_match, axis=1)
    return (route_weight, slot_token, slot_live)


def expert_terms(rows_in, rows_back, weight, gate_cols, up_cols, down_cols):
    gate_pre = jnp.einsum("srk,skh->rh", rows_in, gate_cols, preferred_element_type=jnp.float32)
    up_pre = jnp.einsum("srk,skh->rh", rows_in, up_cols, preferred_element_type=jnp.float32)
    sigmoid_gate = jax.nn.sigmoid(gate_pre)
    active = gate_pre * sigmoid_gate
    back_hidden = weight[:, None] * jnp.einsum(
        "srk,skh->rh", rows_back, down_cols, preferred_element_type=jnp.float32
    )
    scaled = (weight[:, None] * active * up_pre).astype(jnp.bfloat16)
    grad_gate_pre = (
        back_hidden * up_pre * sigmoid_gate * (1.0 + gate_pre * (1.0 - sigmoid_gate))
    ).astype(jnp.bfloat16)
    grad_up_pre = (back_hidden * active).astype(jnp.bfloat16)
    gate_sum = jnp.einsum("srk,rh->skh", rows_in, grad_gate_pre, preferred_element_type=jnp.float32)
    up_sum = jnp.einsum("srk,rh->skh", rows_in, grad_up_pre, preferred_element_type=jnp.float32)
    down_sum = jnp.einsum("srk,rh->skh", rows_back, scaled, preferred_element_type=jnp.float32)
    back = jnp.einsum("rh,skh->srk", grad_gate_pre, gate_cols, preferred_element_type=jnp.float32)
    back = back + jnp.einsum("rh,skh->srk", grad_up_pre, up_cols, preferred_element_type=jnp.float32)
    return (gate_sum, up_sum, down_sum, back)


def on_device(tokens, grad_out, w_gate, w_up, w_down, routing, combine, hot_ids):
    dp_count = lax.axis_size("dp")
    block_rows = tokens.shape[0]
    share_width = tokens.shape[1]
    width = w_gate.shape[1]
    capacity = block_rows * routing.shape[1] // dp_count
    row_index = lax.axis_index("dp")
    hot_expert = hot_ids[0]
    route_weight, slot_token, slot_live = slot_tables(
        routing, combine, hot_expert, dp_count, block_rows, dp_count, capacity
    )
    send_token = slot_token[row_index]
    send_live = slot_live[row_index]
    recv_token = (
        slot_token[:, row_index, :] + (jnp.arange(dp_count, dtype=jnp.int32) * block_rows)[:, None]
    )
    recv_live = slot_live[:, row_index, :]
    cold_weight = jnp.where(
        recv_live, route_weight[recv_token, row_index], jnp.float32(0.0)
    ).reshape(-1)
    block_weight = lax.dynamic_slice_in_dim(route_weight, row_index * block_rows, block_rows, 0)
    hot_weight = block_weight[:, hot_expert]

    share_count = lax.axis_size("expert")
    own = jnp.stack([w_gate[0], w_up[0], w_down[0].T], 0)
    own = own.reshape(3, share_count, width // share_count, own.shape[-1])
    pieces = lax.all_to_all(own, "dp", split_axis=1, concat_axis=1, tiled=True)
    hot_piece = lax.dynamic_index_in_dim(pieces, hot_expert, axis=1, keepdims=False)
    hot_w = lax.all_gather(hot_piece, "dp", axis=1, tiled=True).reshape(own.shape)

    def pack(source):
        picked = jnp.take(source, send_token.reshape(-1), axis=0).reshape(
            dp_count, capacity, source.shape[1]
        )
        return jnp.where(send_live[:, :, None], picked, jnp.zeros_like(picked))

    packed = jnp.concatenate([pack(tokens), pack(grad_out)], 2)
    arrived = lax.all_to_all(packed, "dp", split_axis=0, concat_axis=0, tiled=True)
    arrived_in = arrived[:, :, :share_width].reshape(-1, share_width)
    arrived_back = arrived[:, :, share_width:].reshape(-1, share_width)
    full_in = lax.all_gather(jnp.concatenate([tokens, arrived_in], 0), "expert", axis=0)
    full_back = lax.all_gather(jnp.concatenate([grad_out, arrived_back], 0), "expert", axis=0)
    hot_rows, cold_rows = (full_in[:, :block_rows], full_in[:, block_rows:])
    hot_cotan, cold_cotan = (full_back[:, :block_rows], full_back[:, block_rows:])
    cold_terms = expert_terms(cold_rows, cold_cotan, cold_weight, own[0], own[1], own[2])
    hot_terms = expert_terms(hot_rows, hot_cotan, hot_weight, hot_w[0], hot_w[1], hot_w[2])

    block_sums = jnp.stack([hot_terms[m].astype(jnp.bfloat16) for m in range(3)], 0)
    by_chunk = lax.all_to_all(block_sums, "dp", split_axis=1, concat_axis=1, tiled=True)
    chunk_sum = jnp.sum(by_chunk.astype(jnp.float32), axis=1).astype(jnp.bfloat16)
    summed = lax.all_gather(chunk_sum, "dp", axis=1, tiled=True).reshape(block_sums.shape)
    owns_hot = row_index == hot_expert
    grads = jnp.where(owns_hot, summed, jnp.stack([cold_terms[m] for m in range(3)], 0))
    grads = grads.astype(jnp.bfloat16).reshape(3, width, grads.shape[-1])
    grad_gate, grad_up, grad_down = grads[0], grads[1], grads[2].T

    positions = jnp.arange(block_rows, dtype=jnp.int32)
    select = (positions[:, None] == send_token.reshape(-1)[None, :]) & send_live.reshape(-1)[
        None, :
    ]
    stacked = jnp.concatenate([hot_terms[3], cold_terms[3]], 1)
    shares = lax.psum_scatter(
        stacked.astype(jnp.bfloat16), "expert", scatter_dimension=0, tiled=True
    )[0].astype(jnp.float32)
    hot_share = shares[:block_rows]
    cold_share = shares[block_rows:].reshape(dp_count, capacity, share_width)
    returned = lax.all_to_all(
        cold_share.astype(jnp.bfloat16), "dp", split_axis=0, concat_axis=0, tiled=True
    ).astype(cold_share.dtype)
    gathered_back = jnp.dot(
        select.astype(jnp.float32),
        returned.reshape(-1, share_width),
        precision=lax.Precision.HIGHEST,
        preferred_element_type=jnp.float32,
    )
    token_grad = (hot_share + gathered_back).astype(jnp.bfloat16)
    return (grad_gate[None], grad_up[None], grad_down[None], token_grad)


def solution(mesh):
    return jax.shard_map(
        on_device,
        mesh=mesh,
        in_specs=(
            P("dp", "expert"),
            P("dp", "expert"),
            P("dp", None, "expert"),
            P("dp", None, "expert"),
            P("dp", "expert", None),
            P(),
            P(),
            P(),
        ),
        out_specs=(
            P("dp", None, "expert"),
            P("dp", None, "expert"),
            P("dp", "expert", None),
            P("dp", "expert"),
        ),
        check_vma=False,
    )
```

```python
import jax
import jax.numpy as jnp
from jax import lax
from jax.sharding import PartitionSpec as P


def slot_tables(routing, combine, hot_expert, dp_count, block_rows, expert_count, capacity):
    columns = jnp.arange(expert_count, dtype=jnp.int32)
    name_match = routing[:, :, None] == columns[None, None, :]
    route_weight = jnp.sum(jnp.where(name_match, combine[:, :, None], jnp.float32(0.0)), axis=1)
    named_count = jnp.sum(name_match.astype(jnp.int32), axis=1).reshape(
        dp_count, block_rows, expert_count
    )
    positions = jnp.arange(block_rows, dtype=jnp.int32)
    earlier = (positions[None, :] < positions[:, None]).astype(jnp.bfloat16)
    before = jnp.einsum(
        "ts,bse->bte", earlier, named_count.astype(jnp.bfloat16), preferred_element_type=jnp.float32
    ).astype(jnp.int32)
    slot_ids = jnp.arange(capacity, dtype=jnp.int32)
    slot_match = (
        (named_count[..., None] == 1)
        & (before[..., None] == slot_ids)
        & (columns != hot_expert)[None, None, :, None]
    )
    slot_token = jnp.sum(jnp.where(slot_match, positions[None, :, None, None], 0), axis=1)
    slot_live = jnp.any(slot_match, axis=1)
    return (route_weight, slot_token, slot_live)


def expert_terms(rows_in, rows_back, weight, gate_cols, up_cols, down_cols):
    gate_pre = jnp.einsum("srk,skh->rh", rows_in, gate_cols, preferred_element_type=jnp.float32)
    up_pre = jnp.einsum("srk,skh->rh", rows_in, up_cols, preferred_element_type=jnp.float32)
    sigmoid_gate = jax.nn.sigmoid(gate_pre)
    active = gate_pre * sigmoid_gate
    back_hidden = weight[:, None] * jnp.einsum(
        "srk,skh->rh", rows_back, down_cols, preferred_element_type=jnp.float32
    )
    scaled = (weight[:, None] * active * up_pre).astype(jnp.bfloat16)
    grad_gate_pre = (
        back_hidden * up_pre * sigmoid_gate * (1.0 + gate_pre * (1.0 - sigmoid_gate))
    ).astype(jnp.bfloat16)
    grad_up_pre = (back_hidden * active).astype(jnp.bfloat16)
    gate_sum = jnp.einsum("srk,rh->skh", rows_in, grad_gate_pre, preferred_element_type=jnp.float32)
    up_sum = jnp.einsum("srk,rh->skh", rows_in, grad_up_pre, preferred_element_type=jnp.float32)
    down_sum = jnp.einsum("srk,rh->skh", rows_back, scaled, preferred_element_type=jnp.float32)
    back = jnp.einsum("rh,skh->srk", grad_gate_pre, gate_cols, preferred_element_type=jnp.float32)
    back = back + jnp.einsum("rh,skh->srk", grad_up_pre, up_cols, preferred_element_type=jnp.float32)
    return (gate_sum, up_sum, down_sum, back)


def on_device(tokens, grad_out, w_gate, w_up, w_down, routing, combine, hot_ids):
    dp_count = lax.axis_size("dp")
    block_rows = tokens.shape[0]
    share_width = tokens.shape[1]
    width = w_gate.shape[1]
    capacity = block_rows * routing.shape[1] // dp_count
    row_index = lax.axis_index("dp")
    hot_expert = hot_ids[0]
    route_weight, slot_token, slot_live = slot_tables(
        routing, combine, hot_expert, dp_count, block_rows, dp_count, capacity
    )
    send_token = slot_token[row_index]
    send_live = slot_live[row_index]
    recv_token = (
        slot_token[:, row_index, :] + (jnp.arange(dp_count, dtype=jnp.int32) * block_rows)[:, None]
    )
    recv_live = slot_live[:, row_index, :]
    cold_weight = jnp.where(
        recv_live, route_weight[recv_token, row_index], jnp.float32(0.0)
    ).reshape(-1)
    block_weight = lax.dynamic_slice_in_dim(route_weight, row_index * block_rows, block_rows, 0)
    hot_weight = block_weight[:, hot_expert]

    share_count = lax.axis_size("expert")
    own = jnp.stack([w_gate[0], w_up[0], w_down[0].T], 0)
    own = own.reshape(3, share_count, width // share_count, own.shape[-1])
    pieces = lax.all_to_all(own, "dp", split_axis=1, concat_axis=1, tiled=True)
    hot_piece = lax.dynamic_index_in_dim(pieces, hot_expert, axis=1, keepdims=False)
    hot_w = lax.all_gather(hot_piece, "dp", axis=1, tiled=True).reshape(own.shape)

    def pack(source):
        picked = jnp.take(source, send_token.reshape(-1), axis=0).reshape(
            dp_count, capacity, source.shape[1]
        )
        return jnp.where(send_live[:, :, None], picked, jnp.zeros_like(picked))

    packed = jnp.concatenate([pack(tokens), pack(grad_out)], 2)
    arrived = lax.all_to_all(packed, "dp", split_axis=0, concat_axis=0, tiled=True)
    arrived_in = arrived[:, :, :share_width].reshape(-1, share_width)
    arrived_back = arrived[:, :, share_width:].reshape(-1, share_width)
    local = jnp.stack(
        [jnp.concatenate([tokens, arrived_in], 0), jnp.concatenate([grad_out, arrived_back], 0)], 0
    )
    full = lax.all_gather(local, "expert", axis=1)
    full_in, full_back = full[0], full[1]
    hot_rows, cold_rows = (full_in[:, :block_rows], full_in[:, block_rows:])
    hot_cotan, cold_cotan = (full_back[:, :block_rows], full_back[:, block_rows:])
    cold_terms = expert_terms(cold_rows, cold_cotan, cold_weight, own[0], own[1], own[2])
    hot_terms = expert_terms(hot_rows, hot_cotan, hot_weight, hot_w[0], hot_w[1], hot_w[2])

    block_sums = jnp.stack([hot_terms[m].astype(jnp.bfloat16) for m in range(3)], 0)
    by_chunk = lax.all_to_all(block_sums, "dp", split_axis=1, concat_axis=1, tiled=True)
    chunk_sum = jnp.sum(by_chunk.astype(jnp.float32), axis=1).astype(jnp.bfloat16)
    summed = lax.all_gather(chunk_sum, "dp", axis=1, tiled=True).reshape(block_sums.shape)
    owns_hot = row_index == hot_expert
    grads = jnp.where(owns_hot, summed, jnp.stack([cold_terms[m] for m in range(3)], 0))
    grads = grads.astype(jnp.bfloat16).reshape(3, width, grads.shape[-1])
    grad_gate, grad_up, grad_down = grads[0], grads[1], grads[2].T

    positions = jnp.arange(block_rows, dtype=jnp.int32)
    select = (positions[:, None] == send_token.reshape(-1)[None, :]) & send_live.reshape(-1)[
        None, :
    ]
    stacked = jnp.concatenate([hot_terms[3], cold_terms[3]], 1)
    shares = lax.psum_scatter(
        stacked.astype(jnp.bfloat16), "expert", scatter_dimension=0, tiled=True
    )[0].astype(jnp.float32)
    hot_share = shares[:block_rows]
    cold_share = shares[block_rows:].reshape(dp_count, capacity, share_width)
    returned = lax.all_to_all(
        cold_share.astype(jnp.bfloat16), "dp", split_axis=0, concat_axis=0, tiled=True
    ).astype(cold_share.dtype)
    gathered_back = jnp.dot(
        select.astype(jnp.float32),
        returned.reshape(-1, share_width),
        precision=lax.Precision.HIGHEST,
        preferred_element_type=jnp.float32,
    )
    token_grad = (hot_share + gathered_back).astype(jnp.bfloat16)
    return (grad_gate[None], grad_up[None], grad_down[None], token_grad)


def solution(mesh):
    return jax.shard_map(
        on_device,
        mesh=mesh,
        in_specs=(
            P("dp", "expert"),
            P("dp", "expert"),
            P("dp", None, "expert"),
            P("dp", None, "expert"),
            P("dp", "expert", None),
            P(),
            P(),
            P(),
        ),
        out_specs=(
            P("dp", None, "expert"),
            P("dp", None, "expert"),
            P("dp", "expert", None),
            P("dp", "expert"),
        ),
        check_vma=False,
    )
```

```python
import jax
import jax.numpy as jnp
from jax import lax
from jax.sharding import PartitionSpec as P


def slot_tables(routing, combine, hot_expert, dp_count, block_rows, expert_count, capacity):
    columns = jnp.arange(expert_count, dtype=jnp.int32)
    name_match = routing[:, :, None] == columns[None, None, :]
    route_weight = jnp.sum(jnp.where(name_match, combine[:, :, None], jnp.float32(0.0)), axis=1)
    named_count = jnp.sum(name_match.astype(jnp.int32), axis=1).reshape(
        dp_count, block_rows, expert_count
    )
    positions = jnp.arange(block_rows, dtype=jnp.int32)
    earlier = (positions[None, :] < positions[:, None]).astype(jnp.bfloat16)
    before = jnp.einsum(
        "ts,bse->bte", earlier, named_count.astype(jnp.bfloat16), preferred_element_type=jnp.float32
    ).astype(jnp.int32)
    slot_ids = jnp.arange(capacity, dtype=jnp.int32)
    slot_match = (
        (named_count[..., None] == 1)
        & (before[..., None] == slot_ids)
        & (columns != hot_expert)[None, None, :, None]
    )
    slot_token = jnp.sum(jnp.where(slot_match, positions[None, :, None, None], 0), axis=1)
    slot_live = jnp.any(slot_match, axis=1)
    return (route_weight, slot_token, slot_live)


def expert_terms(rows_in, rows_back, weight, gate_cols, up_cols, down_cols):
    gate_pre = jnp.einsum("srk,skh->rh", rows_in, gate_cols, preferred_element_type=jnp.float32)
    up_pre = jnp.einsum("srk,skh->rh", rows_in, up_cols, preferred_element_type=jnp.float32)
    sigmoid_gate = jax.nn.sigmoid(gate_pre)
    active = gate_pre * sigmoid_gate
    back_hidden = weight[:, None] * jnp.einsum(
        "srk,skh->rh", rows_back, down_cols, preferred_element_type=jnp.float32
    )
    scaled = (weight[:, None] * active * up_pre).astype(jnp.bfloat16)
    grad_gate_pre = (
        back_hidden * up_pre * sigmoid_gate * (1.0 + gate_pre * (1.0 - sigmoid_gate))
    ).astype(jnp.bfloat16)
    grad_up_pre = (back_hidden * active).astype(jnp.bfloat16)
    gate_sum = jnp.einsum("srk,rh->skh", rows_in, grad_gate_pre, preferred_element_type=jnp.float32)
    up_sum = jnp.einsum("srk,rh->skh", rows_in, grad_up_pre, preferred_element_type=jnp.float32)
    down_sum = jnp.einsum("srk,rh->skh", rows_back, scaled, preferred_element_type=jnp.float32)
    back = jnp.einsum("rh,skh->srk", grad_gate_pre, gate_cols, preferred_element_type=jnp.float32)
    back = back + jnp.einsum("rh,skh->srk", grad_up_pre, up_cols, preferred_element_type=jnp.float32)
    return (gate_sum, up_sum, down_sum, back)


def on_device(tokens, grad_out, w_gate, w_up, w_down, routing, combine, hot_ids):
    dp_count = lax.axis_size("dp")
    block_rows = tokens.shape[0]
    share_width = tokens.shape[1]
    width = w_gate.shape[1]
    capacity = block_rows * routing.shape[1] // dp_count
    row_index = lax.axis_index("dp")
    hot_expert = hot_ids[0]
    route_weight, slot_token, slot_live = slot_tables(
        routing, combine, hot_expert, dp_count, block_rows, dp_count, capacity
    )
    send_token = slot_token[row_index]
    send_live = slot_live[row_index]
    recv_token = (
        slot_token[:, row_index, :] + (jnp.arange(dp_count, dtype=jnp.int32) * block_rows)[:, None]
    )
    recv_live = slot_live[:, row_index, :]
    cold_weight = jnp.where(
        recv_live, route_weight[recv_token, row_index], jnp.float32(0.0)
    ).reshape(-1)
    block_weight = lax.dynamic_slice_in_dim(route_weight, row_index * block_rows, block_rows, 0)
    hot_weight = block_weight[:, hot_expert]


    def pack(source):
        picked = jnp.take(source, send_token.reshape(-1), axis=0).reshape(
            dp_count, capacity, source.shape[1]
        )
        return jnp.where(send_live[:, :, None], picked, jnp.zeros_like(picked))

    packed = jnp.concatenate([pack(tokens), pack(grad_out)], 2)
    arrived = lax.all_to_all(packed, "dp", split_axis=0, concat_axis=0, tiled=True)
    arrived_in = arrived[:, :, :share_width].reshape(-1, share_width)
    arrived_back = arrived[:, :, share_width:].reshape(-1, share_width)
    local = jnp.stack(
        [jnp.concatenate([tokens, arrived_in], 0), jnp.concatenate([grad_out, arrived_back], 0)], 0
    )
    share_count = lax.axis_size("expert")
    own = jnp.stack([w_gate[0], w_up[0], w_down[0].T], 0)
    own = own.reshape(3, share_count, width // share_count, own.shape[-1])
    own, local = lax.optimization_barrier((own, local))
    pieces = lax.all_to_all(own, "dp", split_axis=1, concat_axis=1, tiled=True)
    hot_piece = lax.dynamic_index_in_dim(pieces, hot_expert, axis=1, keepdims=False)
    full = lax.all_gather(local, "expert", axis=1)
    hot_piece, full = lax.optimization_barrier((hot_piece, full))
    hot_w = lax.all_gather(hot_piece, "dp", axis=1, tiled=True).reshape(own.shape)
    full_in, full_back = full[0], full[1]
    hot_rows, cold_rows = (full_in[:, :block_rows], full_in[:, block_rows:])
    hot_cotan, cold_cotan = (full_back[:, :block_rows], full_back[:, block_rows:])
    cold_terms = expert_terms(cold_rows, cold_cotan, cold_weight, own[0], own[1], own[2])
    hot_terms = expert_terms(hot_rows, hot_cotan, hot_weight, hot_w[0], hot_w[1], hot_w[2])

    block_sums = jnp.stack([hot_terms[m].astype(jnp.bfloat16) for m in range(3)], 0)
    by_chunk = lax.all_to_all(block_sums, "dp", split_axis=1, concat_axis=1, tiled=True)
    chunk_sum = jnp.sum(by_chunk.astype(jnp.float32), axis=1).astype(jnp.bfloat16)
    summed = lax.all_gather(chunk_sum, "dp", axis=1, tiled=True).reshape(block_sums.shape)
    owns_hot = row_index == hot_expert
    grads = jnp.where(owns_hot, summed, jnp.stack([cold_terms[m] for m in range(3)], 0))
    grads = grads.astype(jnp.bfloat16).reshape(3, width, grads.shape[-1])
    grad_gate, grad_up, grad_down = grads[0], grads[1], grads[2].T

    positions = jnp.arange(block_rows, dtype=jnp.int32)
    select = (positions[:, None] == send_token.reshape(-1)[None, :]) & send_live.reshape(-1)[
        None, :
    ]
    stacked = jnp.concatenate([hot_terms[3], cold_terms[3]], 1)
    shares = lax.psum_scatter(
        stacked.astype(jnp.bfloat16), "expert", scatter_dimension=0, tiled=True
    )[0].astype(jnp.float32)
    hot_share = shares[:block_rows]
    cold_share = shares[block_rows:].reshape(dp_count, capacity, share_width)
    returned = lax.all_to_all(
        cold_share.astype(jnp.bfloat16), "dp", split_axis=0, concat_axis=0, tiled=True
    ).astype(cold_share.dtype)
    gathered_back = jnp.dot(
        select.astype(jnp.float32),
        returned.reshape(-1, share_width),
        precision=lax.Precision.HIGHEST,
        preferred_element_type=jnp.float32,
    )
    token_grad = (hot_share + gathered_back).astype(jnp.bfloat16)
    return (grad_gate[None], grad_up[None], grad_down[None], token_grad)


def solution(mesh):
    return jax.shard_map(
        on_device,
        mesh=mesh,
        in_specs=(
            P("dp", "expert"),
            P("dp", "expert"),
            P("dp", None, "expert"),
            P("dp", None, "expert"),
            P("dp", "expert", None),
            P(),
            P(),
            P(),
        ),
        out_specs=(
            P("dp", None, "expert"),
            P("dp", None, "expert"),
            P("dp", "expert", None),
            P("dp", "expert"),
        ),
        check_vma=False,
    )
```

```python
import jax
import jax.numpy as jnp
from jax import lax
from jax.sharding import PartitionSpec as P


def slot_tables(routing, combine, hot_expert, dp_count, block_rows, expert_count, capacity):
    columns = jnp.arange(expert_count, dtype=jnp.int32)
    name_match = routing[:, :, None] == columns[None, None, :]
    route_weight = jnp.sum(jnp.where(name_match, combine[:, :, None], jnp.float32(0.0)), axis=1)
    named_count = jnp.sum(name_match.astype(jnp.int32), axis=1).reshape(
        dp_count, block_rows, expert_count
    )
    positions = jnp.arange(block_rows, dtype=jnp.int32)
    earlier = (positions[None, :] < positions[:, None]).astype(jnp.bfloat16)
    before = jnp.einsum(
        "ts,bse->bte", earlier, named_count.astype(jnp.bfloat16), preferred_element_type=jnp.float32
    ).astype(jnp.int32)
    slot_ids = jnp.arange(capacity, dtype=jnp.int32)
    slot_match = (
        (named_count[..., None] == 1)
        & (before[..., None] == slot_ids)
        & (columns != hot_expert)[None, None, :, None]
    )
    slot_token = jnp.sum(jnp.where(slot_match, positions[None, :, None, None], 0), axis=1)
    slot_live = jnp.any(slot_match, axis=1)
    return (route_weight, slot_token, slot_live)


def expert_terms(rows_in, rows_back, weight, gate_cols, up_cols, down_cols):
    gate_pre = jnp.einsum("srk,skh->rh", rows_in, gate_cols, preferred_element_type=jnp.float32)
    up_pre = jnp.einsum("srk,skh->rh", rows_in, up_cols, preferred_element_type=jnp.float32)
    sigmoid_gate = jax.nn.sigmoid(gate_pre)
    active = gate_pre * sigmoid_gate
    back_hidden = weight[:, None] * jnp.einsum(
        "srk,skh->rh", rows_back, down_cols, preferred_element_type=jnp.float32
    )
    scaled = (weight[:, None] * active * up_pre).astype(jnp.bfloat16)
    grad_gate_pre = (
        back_hidden * up_pre * sigmoid_gate * (1.0 + gate_pre * (1.0 - sigmoid_gate))
    ).astype(jnp.bfloat16)
    grad_up_pre = (back_hidden * active).astype(jnp.bfloat16)
    gate_sum = jnp.einsum("srk,rh->skh", rows_in, grad_gate_pre, preferred_element_type=jnp.float32)
    up_sum = jnp.einsum("srk,rh->skh", rows_in, grad_up_pre, preferred_element_type=jnp.float32)
    down_sum = jnp.einsum("srk,rh->skh", rows_back, scaled, preferred_element_type=jnp.float32)
    back = jnp.einsum("rh,skh->srk", grad_gate_pre, gate_cols, preferred_element_type=jnp.float32)
    back = back + jnp.einsum("rh,skh->srk", grad_up_pre, up_cols, preferred_element_type=jnp.float32)
    return (gate_sum, up_sum, down_sum, back)


def on_device(tokens, grad_out, w_gate, w_up, w_down, routing, combine, hot_ids):
    dp_count = lax.axis_size("dp")
    block_rows = tokens.shape[0]
    share_width = tokens.shape[1]
    width = w_gate.shape[1]
    capacity = block_rows * routing.shape[1] // dp_count
    row_index = lax.axis_index("dp")
    hot_expert = hot_ids[0]
    route_weight, slot_token, slot_live = slot_tables(
        routing, combine, hot_expert, dp_count, block_rows, dp_count, capacity
    )
    send_token = slot_token[row_index]
    send_live = slot_live[row_index]
    recv_token = (
        slot_token[:, row_index, :] + (jnp.arange(dp_count, dtype=jnp.int32) * block_rows)[:, None]
    )
    recv_live = slot_live[:, row_index, :]
    cold_weight = jnp.where(
        recv_live, route_weight[recv_token, row_index], jnp.float32(0.0)
    ).reshape(-1)
    block_weight = lax.dynamic_slice_in_dim(route_weight, row_index * block_rows, block_rows, 0)
    hot_weight = block_weight[:, hot_expert]

    share_count = lax.axis_size("expert")
    own = jnp.stack([w_gate[0], w_up[0], w_down[0].T], 0)
    own = own.reshape(3, share_count, width // share_count, own.shape[-1])
    pieces = lax.all_to_all(own, "dp", split_axis=1, concat_axis=1, tiled=True)
    hot_piece = lax.dynamic_index_in_dim(pieces, hot_expert, axis=1, keepdims=False)
    copies = jnp.broadcast_to(hot_piece[:, None], own.shape)
    hot_w = lax.all_to_all(copies, "dp", split_axis=1, concat_axis=1, tiled=True)

    def pack(source):
        picked = jnp.take(source, send_token.reshape(-1), axis=0).reshape(
            dp_count, capacity, source.shape[1]
        )
        return jnp.where(send_live[:, :, None], picked, jnp.zeros_like(picked))

    packed = jnp.concatenate([pack(tokens), pack(grad_out)], 2)
    arrived = lax.all_to_all(packed, "dp", split_axis=0, concat_axis=0, tiled=True)
    arrived_in = arrived[:, :, :share_width].reshape(-1, share_width)
    arrived_back = arrived[:, :, share_width:].reshape(-1, share_width)
    full_in = lax.all_gather(jnp.concatenate([tokens, arrived_in], 0), "expert", axis=0)
    full_back = lax.all_gather(jnp.concatenate([grad_out, arrived_back], 0), "expert", axis=0)
    hot_rows, cold_rows = (full_in[:, :block_rows], full_in[:, block_rows:])
    hot_cotan, cold_cotan = (full_back[:, :block_rows], full_back[:, block_rows:])
    cold_terms = expert_terms(cold_rows, cold_cotan, cold_weight, own[0], own[1], own[2])
    hot_terms = expert_terms(hot_rows, hot_cotan, hot_weight, hot_w[0], hot_w[1], hot_w[2])

    block_sums = jnp.stack([hot_terms[m].astype(jnp.bfloat16) for m in range(3)], 0)
    by_chunk = lax.all_to_all(block_sums, "dp", split_axis=1, concat_axis=1, tiled=True)
    chunk_sum = jnp.sum(by_chunk.astype(jnp.float32), axis=1).astype(jnp.bfloat16)
    summed = lax.all_gather(chunk_sum, "dp", axis=1, tiled=True).reshape(block_sums.shape)
    owns_hot = row_index == hot_expert
    grads = jnp.where(owns_hot, summed, jnp.stack([cold_terms[m] for m in range(3)], 0))
    grads = grads.astype(jnp.bfloat16).reshape(3, width, grads.shape[-1])
    grad_gate, grad_up, grad_down = grads[0], grads[1], grads[2].T

    positions = jnp.arange(block_rows, dtype=jnp.int32)
    select = (positions[:, None] == send_token.reshape(-1)[None, :]) & send_live.reshape(-1)[
        None, :
    ]
    stacked = jnp.concatenate([hot_terms[3], cold_terms[3]], 1)
    shares = lax.psum_scatter(
        stacked.astype(jnp.bfloat16), "expert", scatter_dimension=0, tiled=True
    )[0].astype(jnp.float32)
    hot_share = shares[:block_rows]
    cold_share = shares[block_rows:].reshape(dp_count, capacity, share_width)
    returned = lax.all_to_all(
        cold_share.astype(jnp.bfloat16), "dp", split_axis=0, concat_axis=0, tiled=True
    ).astype(cold_share.dtype)
    gathered_back = jnp.dot(
        select.astype(jnp.float32),
        returned.reshape(-1, share_width),
        precision=lax.Precision.HIGHEST,
        preferred_element_type=jnp.float32,
    )
    token_grad = (hot_share + gathered_back).astype(jnp.bfloat16)
    return (grad_gate[None], grad_up[None], grad_down[None], token_grad)


def solution(mesh):
    return jax.shard_map(
        on_device,
        mesh=mesh,
        in_specs=(
            P("dp", "expert"),
            P("dp", "expert"),
            P("dp", None, "expert"),
            P("dp", None, "expert"),
            P("dp", "expert", None),
            P(),
            P(),
            P(),
        ),
        out_specs=(
            P("dp", None, "expert"),
            P("dp", None, "expert"),
            P("dp", "expert", None),
            P("dp", "expert"),
        ),
        check_vma=False,
    )
```

```python
import jax
import jax.numpy as jnp
from jax import lax
from jax.sharding import PartitionSpec as P


def slot_tables(routing, combine, hot_expert, dp_count, block_rows, expert_count, capacity):
    columns = jnp.arange(expert_count, dtype=jnp.int32)
    name_match = routing[:, :, None] == columns[None, None, :]
    route_weight = jnp.sum(jnp.where(name_match, combine[:, :, None], jnp.float32(0.0)), axis=1)
    named_count = jnp.sum(name_match.astype(jnp.int32), axis=1).reshape(
        dp_count, block_rows, expert_count
    )
    positions = jnp.arange(block_rows, dtype=jnp.int32)
    earlier = (positions[None, :] < positions[:, None]).astype(jnp.bfloat16)
    before = jnp.einsum(
        "ts,bse->bte", earlier, named_count.astype(jnp.bfloat16), preferred_element_type=jnp.float32
    ).astype(jnp.int32)
    slot_ids = jnp.arange(capacity, dtype=jnp.int32)
    slot_match = (
        (named_count[..., None] == 1)
        & (before[..., None] == slot_ids)
        & (columns != hot_expert)[None, None, :, None]
    )
    slot_token = jnp.sum(jnp.where(slot_match, positions[None, :, None, None], 0), axis=1)
    slot_live = jnp.any(slot_match, axis=1)
    return (route_weight, slot_token, slot_live)


def expert_terms(rows_in, rows_back, weight, gate_cols, up_cols, down_cols):
    gate_pre = jnp.einsum("srk,skh->rh", rows_in, gate_cols, preferred_element_type=jnp.float32)
    up_pre = jnp.einsum("srk,skh->rh", rows_in, up_cols, preferred_element_type=jnp.float32)
    sigmoid_gate = jax.nn.sigmoid(gate_pre)
    active = gate_pre * sigmoid_gate
    back_hidden = weight[:, None] * jnp.einsum(
        "srk,skh->rh", rows_back, down_cols, preferred_element_type=jnp.float32
    )
    scaled = (weight[:, None] * active * up_pre).astype(jnp.bfloat16)
    grad_gate_pre = (
        back_hidden * up_pre * sigmoid_gate * (1.0 + gate_pre * (1.0 - sigmoid_gate))
    ).astype(jnp.bfloat16)
    grad_up_pre = (back_hidden * active).astype(jnp.bfloat16)
    gate_sum = jnp.einsum("srk,rh->skh", rows_in, grad_gate_pre, preferred_element_type=jnp.float32)
    up_sum = jnp.einsum("srk,rh->skh", rows_in, grad_up_pre, preferred_element_type=jnp.float32)
    down_sum = jnp.einsum("srk,rh->skh", rows_back, scaled, preferred_element_type=jnp.float32)
    back = jnp.einsum("rh,skh->srk", grad_gate_pre, gate_cols, preferred_element_type=jnp.float32)
    back = back + jnp.einsum("rh,skh->srk", grad_up_pre, up_cols, preferred_element_type=jnp.float32)
    return (gate_sum, up_sum, down_sum, back)


def on_device(tokens, grad_out, w_gate, w_up, w_down, routing, combine, hot_ids):
    dp_count = lax.axis_size("dp")
    block_rows = tokens.shape[0]
    share_width = tokens.shape[1]
    width = w_gate.shape[1]
    capacity = block_rows * routing.shape[1] // dp_count
    row_index = lax.axis_index("dp")
    hot_expert = hot_ids[0]
    route_weight, slot_token, slot_live = slot_tables(
        routing, combine, hot_expert, dp_count, block_rows, dp_count, capacity
    )
    send_token = slot_token[row_index]
    send_live = slot_live[row_index]
    recv_token = (
        slot_token[:, row_index, :] + (jnp.arange(dp_count, dtype=jnp.int32) * block_rows)[:, None]
    )
    recv_live = slot_live[:, row_index, :]
    cold_weight = jnp.where(
        recv_live, route_weight[recv_token, row_index], jnp.float32(0.0)
    ).reshape(-1)
    block_weight = lax.dynamic_slice_in_dim(route_weight, row_index * block_rows, block_rows, 0)
    hot_weight = block_weight[:, hot_expert]

    share_count = lax.axis_size("expert")
    own = jnp.stack([w_gate[0], w_up[0], w_down[0].T], 0)
    own = own.reshape(3, share_count, width // share_count, own.shape[-1])
    pieces = lax.all_to_all(own, "dp", split_axis=1, concat_axis=1, tiled=True)
    hot_piece = lax.dynamic_index_in_dim(pieces, hot_expert, axis=1, keepdims=False)
    copies = jnp.broadcast_to(hot_piece[:, None], own.shape)
    hot_w = lax.all_to_all(copies, "dp", split_axis=1, concat_axis=1, tiled=True)

    def pack(source):
        picked = jnp.take(source, send_token.reshape(-1), axis=0).reshape(
            dp_count, capacity, source.shape[1]
        )
        return jnp.where(send_live[:, :, None], picked, jnp.zeros_like(picked))

    packed = jnp.concatenate([pack(tokens), pack(grad_out)], 2)
    arrived = lax.all_to_all(packed, "dp", split_axis=0, concat_axis=0, tiled=True)
    arrived_in = arrived[:, :, :share_width].reshape(-1, share_width)
    arrived_back = arrived[:, :, share_width:].reshape(-1, share_width)
    local = jnp.stack(
        [jnp.concatenate([tokens, arrived_in], 0), jnp.concatenate([grad_out, arrived_back], 0)], 0
    )
    full = lax.all_gather(local, "expert", axis=1)
    full_in, full_back = full[0], full[1]
    hot_rows, cold_rows = (full_in[:, :block_rows], full_in[:, block_rows:])
    hot_cotan, cold_cotan = (full_back[:, :block_rows], full_back[:, block_rows:])
    cold_terms = expert_terms(cold_rows, cold_cotan, cold_weight, own[0], own[1], own[2])
    hot_terms = expert_terms(hot_rows, hot_cotan, hot_weight, hot_w[0], hot_w[1], hot_w[2])

    block_sums = jnp.stack([hot_terms[m].astype(jnp.bfloat16) for m in range(3)], 0)
    by_chunk = lax.all_to_all(block_sums, "dp", split_axis=1, concat_axis=1, tiled=True)
    chunk_sum = jnp.sum(by_chunk.astype(jnp.float32), axis=1).astype(jnp.bfloat16)
    summed = lax.all_gather(chunk_sum, "dp", axis=1, tiled=True).reshape(block_sums.shape)
    owns_hot = row_index == hot_expert
    grads = jnp.where(owns_hot, summed, jnp.stack([cold_terms[m] for m in range(3)], 0))
    grads = grads.astype(jnp.bfloat16).reshape(3, width, grads.shape[-1])
    grad_gate, grad_up, grad_down = grads[0], grads[1], grads[2].T

    positions = jnp.arange(block_rows, dtype=jnp.int32)
    select = (positions[:, None] == send_token.reshape(-1)[None, :]) & send_live.reshape(-1)[
        None, :
    ]
    stacked = jnp.concatenate([hot_terms[3], cold_terms[3]], 1)
    shares = lax.psum_scatter(
        stacked.astype(jnp.bfloat16), "expert", scatter_dimension=0, tiled=True
    )[0].astype(jnp.float32)
    hot_share = shares[:block_rows]
    cold_share = shares[block_rows:].reshape(dp_count, capacity, share_width)
    returned = lax.all_to_all(
        cold_share.astype(jnp.bfloat16), "dp", split_axis=0, concat_axis=0, tiled=True
    ).astype(cold_share.dtype)
    gathered_back = jnp.dot(
        select.astype(jnp.float32),
        returned.reshape(-1, share_width),
        precision=lax.Precision.HIGHEST,
        preferred_element_type=jnp.float32,
    )
    token_grad = (hot_share + gathered_back).astype(jnp.bfloat16)
    return (grad_gate[None], grad_up[None], grad_down[None], token_grad)


def solution(mesh):
    return jax.shard_map(
        on_device,
        mesh=mesh,
        in_specs=(
            P("dp", "expert"),
            P("dp", "expert"),
            P("dp", None, "expert"),
            P("dp", None, "expert"),
            P("dp", "expert", None),
            P(),
            P(),
            P(),
        ),
        out_specs=(
            P("dp", None, "expert"),
            P("dp", None, "expert"),
            P("dp", "expert", None),
            P("dp", "expert"),
        ),
        check_vma=False,
    )
```

```python
import functools

import jax
import jax.numpy as jnp
from jax import lax
from jax.sharding import PartitionSpec as P


def slot_tables(routing, combine, hot_expert, dp_count, block_rows, expert_count, capacity):
    columns = jnp.arange(expert_count, dtype=jnp.int32)
    name_match = routing[:, :, None] == columns[None, None, :]
    route_weight = jnp.sum(jnp.where(name_match, combine[:, :, None], jnp.float32(0.0)), axis=1)
    named_count = jnp.sum(name_match.astype(jnp.int32), axis=1).reshape(
        dp_count, block_rows, expert_count
    )
    positions = jnp.arange(block_rows, dtype=jnp.int32)
    earlier = (positions[None, :] < positions[:, None]).astype(jnp.bfloat16)
    before = jnp.einsum(
        "ts,bse->bte", earlier, named_count.astype(jnp.bfloat16), preferred_element_type=jnp.float32
    ).astype(jnp.int32)
    slot_ids = jnp.arange(capacity, dtype=jnp.int32)
    slot_match = (
        (named_count[..., None] == 1)
        & (before[..., None] == slot_ids)
        & (columns != hot_expert)[None, None, :, None]
    )
    slot_token = jnp.sum(jnp.where(slot_match, positions[None, :, None, None], 0), axis=1)
    slot_live = jnp.any(slot_match, axis=1)
    return (route_weight, slot_token, slot_live)


def expert_terms(rows_in, rows_back, weight, gate_cols, up_cols, down_cols):
    gate_pre = jnp.einsum("srk,skh->rh", rows_in, gate_cols, preferred_element_type=jnp.float32)
    up_pre = jnp.einsum("srk,skh->rh", rows_in, up_cols, preferred_element_type=jnp.float32)
    sigmoid_gate = jax.nn.sigmoid(gate_pre)
    active = gate_pre * sigmoid_gate
    back_hidden = weight[:, None] * jnp.einsum(
        "srk,skh->rh", rows_back, down_cols, preferred_element_type=jnp.float32
    )
    scaled = (weight[:, None] * active * up_pre).astype(jnp.bfloat16)
    grad_gate_pre = (
        back_hidden * up_pre * sigmoid_gate * (1.0 + gate_pre * (1.0 - sigmoid_gate))
    ).astype(jnp.bfloat16)
    grad_up_pre = (back_hidden * active).astype(jnp.bfloat16)
    gate_sum = jnp.einsum("srk,rh->skh", rows_in, grad_gate_pre, preferred_element_type=jnp.float32)
    up_sum = jnp.einsum("srk,rh->skh", rows_in, grad_up_pre, preferred_element_type=jnp.float32)
    down_sum = jnp.einsum("srk,rh->skh", rows_back, scaled, preferred_element_type=jnp.float32)
    back = jnp.einsum("rh,skh->srk", grad_gate_pre, gate_cols, preferred_element_type=jnp.float32)
    back = back + jnp.einsum("rh,skh->srk", grad_up_pre, up_cols, preferred_element_type=jnp.float32)
    return (gate_sum, up_sum, down_sum, back)


def scatter_from(owner, own):
    index = lax.axis_index("dp")
    bits = own.shape[1].bit_length() - 1
    held = own.reshape(own.shape[:1] + (2,) * bits + own.shape[2:])
    axis_of = {bit: bits - bit for bit in range(bits)}
    holders = {owner}
    for bit in sorted(range(bits), key=lambda b: (b != 0, b == 1, b)):
        axis = axis_of.pop(bit)
        mine = (index >> bit) & 1
        keep = lax.dynamic_index_in_dim(held, mine, axis=axis, keepdims=False)
        send = lax.dynamic_index_in_dim(held, 1 - mine, axis=axis, keepdims=False)
        got = lax.ppermute(send, "dp", [(h, h ^ (1 << bit)) for h in sorted(holders)])
        held = jnp.where(((index ^ owner) >> bit) & 1 == 1, got, keep)
        holders |= {h ^ (1 << bit) for h in holders}
        axis_of = {b: a - (a > axis) for b, a in axis_of.items()}
    return held.reshape(own.shape[:1] + own.shape[2:])


def on_device(tokens, grad_out, w_gate, w_up, w_down, routing, combine, hot_ids):
    dp_count = lax.axis_size("dp")
    block_rows = tokens.shape[0]
    share_width = tokens.shape[1]
    width = w_gate.shape[1]
    capacity = block_rows * routing.shape[1] // dp_count
    row_index = lax.axis_index("dp")
    hot_expert = hot_ids[0]
    route_weight, slot_token, slot_live = slot_tables(
        routing, combine, hot_expert, dp_count, block_rows, dp_count, capacity
    )
    send_token = slot_token[row_index]
    send_live = slot_live[row_index]
    recv_token = (
        slot_token[:, row_index, :] + (jnp.arange(dp_count, dtype=jnp.int32) * block_rows)[:, None]
    )
    recv_live = slot_live[:, row_index, :]
    cold_weight = jnp.where(
        recv_live, route_weight[recv_token, row_index], jnp.float32(0.0)
    ).reshape(-1)
    block_weight = lax.dynamic_slice_in_dim(route_weight, row_index * block_rows, block_rows, 0)
    hot_weight = block_weight[:, hot_expert]

    share_count = lax.axis_size("expert")
    own = jnp.stack([w_gate[0], w_up[0], w_down[0].T], 0)
    own = own.reshape(3, share_count, width // share_count, own.shape[-1])
    hot_piece = lax.switch(
        hot_expert, [functools.partial(scatter_from, owner) for owner in range(dp_count)], own
    )
    copies = jnp.broadcast_to(hot_piece[:, None], own.shape)
    hot_w = lax.all_to_all(copies, "dp", split_axis=1, concat_axis=1, tiled=True)

    def pack(source):
        picked = jnp.take(source, send_token.reshape(-1), axis=0).reshape(
            dp_count, capacity, source.shape[1]
        )
        return jnp.where(send_live[:, :, None], picked, jnp.zeros_like(picked))

    packed = jnp.concatenate([pack(tokens), pack(grad_out)], 2)
    arrived = lax.all_to_all(packed, "dp", split_axis=0, concat_axis=0, tiled=True)
    arrived_in = arrived[:, :, :share_width].reshape(-1, share_width)
    arrived_back = arrived[:, :, share_width:].reshape(-1, share_width)
    full_in = lax.all_gather(jnp.concatenate([tokens, arrived_in], 0), "expert", axis=0)
    full_back = lax.all_gather(jnp.concatenate([grad_out, arrived_back], 0), "expert", axis=0)
    hot_rows, cold_rows = (full_in[:, :block_rows], full_in[:, block_rows:])
    hot_cotan, cold_cotan = (full_back[:, :block_rows], full_back[:, block_rows:])
    cold_terms = expert_terms(cold_rows, cold_cotan, cold_weight, own[0], own[1], own[2])
    hot_terms = expert_terms(hot_rows, hot_cotan, hot_weight, hot_w[0], hot_w[1], hot_w[2])

    block_sums = jnp.stack([hot_terms[m].astype(jnp.bfloat16) for m in range(3)], 0)
    by_chunk = lax.all_to_all(block_sums, "dp", split_axis=1, concat_axis=1, tiled=True)
    chunk_sum = jnp.sum(by_chunk.astype(jnp.float32), axis=1).astype(jnp.bfloat16)
    summed = lax.all_gather(chunk_sum, "dp", axis=1, tiled=True).reshape(block_sums.shape)
    owns_hot = row_index == hot_expert
    grads = jnp.where(owns_hot, summed, jnp.stack([cold_terms[m] for m in range(3)], 0))
    grads = grads.astype(jnp.bfloat16).reshape(3, width, grads.shape[-1])
    grad_gate, grad_up, grad_down = grads[0], grads[1], grads[2].T

    positions = jnp.arange(block_rows, dtype=jnp.int32)
    select = (positions[:, None] == send_token.reshape(-1)[None, :]) & send_live.reshape(-1)[
        None, :
    ]
    stacked = jnp.concatenate([hot_terms[3], cold_terms[3]], 1)
    shares = lax.psum_scatter(
        stacked.astype(jnp.bfloat16), "expert", scatter_dimension=0, tiled=True
    )[0].astype(jnp.float32)
    hot_share = shares[:block_rows]
    cold_share = shares[block_rows:].reshape(dp_count, capacity, share_width)
    returned = lax.all_to_all(
        cold_share.astype(jnp.bfloat16), "dp", split_axis=0, concat_axis=0, tiled=True
    ).astype(cold_share.dtype)
    gathered_back = jnp.dot(
        select.astype(jnp.float32),
        returned.reshape(-1, share_width),
        precision=lax.Precision.HIGHEST,
        preferred_element_type=jnp.float32,
    )
    token_grad = (hot_share + gathered_back).astype(jnp.bfloat16)
    return (grad_gate[None], grad_up[None], grad_down[None], token_grad)


def solution(mesh):
    return jax.shard_map(
        on_device,
        mesh=mesh,
        in_specs=(
            P("dp", "expert"),
            P("dp", "expert"),
            P("dp", None, "expert"),
            P("dp", None, "expert"),
            P("dp", "expert", None),
            P(),
            P(),
            P(),
        ),
        out_specs=(
            P("dp", None, "expert"),
            P("dp", None, "expert"),
            P("dp", "expert", None),
            P("dp", "expert"),
        ),
        check_vma=False,
    )
```
